32 devices in a mesh: fsdp: 8 (over y, x, core), ep: 4 (over z).
Axes of the slice: x: 2, y: 2, z: 4, core: 2. Of those that a mesh axis runs over, the one named last changes fastest.
Arguments:
- hidden: bfloat16 [2048, 8192], P('fsdp', 'ep'), may hold values from -6 to 6
- w_down: bfloat16 [6144, 2, 8192], P('fsdp', None, 'ep'), may hold values from -0.0625 to 0.0625
- route_ids: int32 [1024, 2], P('fsdp'), may hold values from 0 to 7, as said below
- probs: float32 [1024, 2], P('fsdp'), may hold values from 0.1 to 0.9
- grad_out: bfloat16 [1024, 6144], P('fsdp', 'ep'), may hold values from -6 to 6
Outputs:
- output: bfloat16 [1024, 6144], P('fsdp', 'ep')
- grad_hidden: bfloat16 [2048, 8192], P('fsdp', 'ep')
- grad_weight: bfloat16 [6144, 2, 8192], P('fsdp', None, 'ep')
- grad_probs: float32 [1024, 2], P('fsdp')
The draws below stay inside these ranges and needn't reach their ends.
Inputs may be any that keep to these rules, and one draw needn't show every extreme that they name: `route_ids`: each token names 2 different experts. Within one panel's 128 tokens, experts 0 and 1 are each named by 1 to 128 tokens, and in some panel both are named by all 128 tokens.
All inputs are finite; a program needn't handle non-finite values.
Results may differ from the reference program's by a relative error of at most 0.012.
Values may be sent and summed in bfloat16 or wider, within the bound.
A program may use at most 384 MiB of HBM per device.

```python
import jax
import jax.numpy as jnp
from jax import lax

D = 6144
FF = 8192
EXPERTS = 8
EXP_WIN = 2
TOP = 2
BLOCK = 128
TOK_DEV = 128
NBLK = 2
ROWS = 256
TOKENS = 1024
N_FSDP = 8
N_EP = 4


def draw_route_ids(key, part):
    panels = TOKENS // TOK_DEV
    keys = jax.random.split(key, 7)
    counts = jax.random.randint(keys[0], (panels, 2), 1, TOK_DEV + 1)
    full_both = jax.random.randint(keys[1], (), 0, panels)
    counts = counts.at[full_both, 0].set(TOK_DEV).at[full_both, 1].set(TOK_DEV)
    order_keys = jax.random.split(keys[3], panels * 2)
    orders = jax.vmap(lambda single: jax.random.permutation(single, TOK_DEV))(order_keys).reshape(panels, 2, TOK_DEV)
    ranks = jnp.argsort(orders, axis=2)
    member = ranks < counts[:, :, None]
    in_zero = member[:, 0]
    in_one = member[:, 1]
    first_fill = jax.random.randint(keys[4], (panels, TOK_DEV), 2, EXPERTS)
    step_fill = jax.random.randint(keys[5], (panels, TOK_DEV), 1, EXPERTS - 2)
    second_fill = 2 + (first_fill - 2 + step_fill) % (EXPERTS - 2)
    flip = jax.random.randint(keys[6], (panels, TOK_DEV), 0, 2)
    first_pick = jnp.where(in_zero, 0, jnp.where(in_one, 1, first_fill))
    second_pick = jnp.where(in_zero & in_one, 1, jnp.where(in_zero | in_one, first_fill, second_fill))
    slot_first = jnp.where(flip == 1, second_pick, first_pick)
    slot_second = jnp.where(flip == 1, first_pick, second_pick)
    return jnp.stack([slot_first, slot_second], axis=2).reshape(TOKENS, 2).astype(jnp.int32)


def block_scale(own_key, extent, shards, least, largest):
    gain = 1.0
    for position, blocks in shards:
        draws = jax.random.uniform(jax.random.fold_in(jax.random.fold_in(own_key, 6), position), (blocks,), jnp.float32, least / len(shards), largest / len(shards))
        gain = gain * jnp.repeat(jnp.exp(draws), extent[position] // blocks).reshape((-1,) + (1,) * (len(extent) - 1 - position))
    return gain


def gaussian(rng, dims, width, reach, cuts=(), kind=jnp.bfloat16):
    array = width * jax.random.normal(rng, dims, jnp.float32)
    if cuts:
        array = array * block_scale(rng, dims, cuts, -0.22, 0.18)
    return jnp.clip(array, -reach, reach).astype(kind)


def setup_inputs(seed: int = 0) -> dict:
    seeds = jax.random.split(jax.random.key(seed), 6)
    hidden = gaussian(seeds[0], (N_FSDP * ROWS, FF), 1.0, 6.0, ((0, 8), (1, 4)))
    w_down = gaussian(seeds[1], (D, EXP_WIN, FF), FF ** -0.5, 0.0625, ((0, 8), (2, 4)))
    route_ids = draw_route_ids(jax.random.fold_in(seeds[5], 71), 0)
    probs = jnp.clip(0.1 + 0.79999997 * jax.random.uniform(seeds[3], (TOKENS, TOP), jnp.float32) ** block_scale(seeds[3], (TOKENS, TOP), ((0, 8),), -0.2, 0.2), 0.1, 0.9)
    grad_out = gaussian(seeds[4], (TOKENS, D), 1.0, 6.0, ((0, 8), (1, 4)))
    return {"hidden": hidden, "w_down": w_down, "route_ids": route_ids, "probs": probs, "grad_out": grad_out}


def route_layout(route_part, prob_part, expert_count, block_rows, row_count):
    token_count = route_part.shape[0]
    experts = jnp.arange(expert_count, dtype=jnp.int32)
    hits = (route_part[:, :, None] == experts[None, None, :]).astype(jnp.int32)
    named = jnp.sum(hits, axis=1).astype(jnp.int32)
    counts = jnp.sum(named, axis=0).astype(jnp.int32)
    ranks = (jnp.cumsum(named, axis=0) - named).astype(jnp.int32)
    padded = (((counts + block_rows - 1) // block_rows) * block_rows).astype(jnp.int32)
    offsets = (jnp.cumsum(padded) - padded).astype(jnp.int32)
    row_of = jnp.sum(hits * (offsets[None, None, :] + ranks[:, None, :]), axis=2).astype(jnp.int32)
    valid = jnp.sum(hits, axis=2).astype(jnp.int32)
    starts = jnp.arange(row_count // block_rows, dtype=jnp.int32) * block_rows
    inside = (starts[:, None] >= offsets[None, :]) & (starts[:, None] < (offsets + padded)[None, :])
    block_exp = (jnp.sum(jnp.where(inside, experts[None, :] + 1, 0), axis=1) - 1).astype(jnp.int32)
    target = jnp.where(valid > 0, row_of, row_count).reshape(-1).astype(jnp.int32)
    token_index = jnp.broadcast_to(jnp.arange(token_count, dtype=jnp.int32)[:, None], route_part.shape).reshape(-1)
    row_tok = jnp.zeros((row_count,), jnp.int32).at[target].set(token_index, mode="drop")
    row_live = jnp.zeros((row_count,), jnp.int32).at[target].set(jnp.ones_like(token_index), mode="drop")
    row_prob = jnp.zeros((row_count,), prob_part.dtype).at[target].set(prob_part.reshape(-1), mode="drop")
    return row_of, valid, block_exp, row_tok, row_live, row_prob


def reference(hidden, w_down, route_ids, probs, grad_out):
    model_width = w_down.shape[0]
    expert_count = w_down.shape[1]
    unit_count = w_down.shape[2]
    group = unit_count // N_EP
    hidden_all = hidden.reshape(N_FSDP, ROWS, unit_count)
    route_all = route_ids.reshape(N_FSDP, TOK_DEV, TOP)
    prob_all = probs.reshape(N_FSDP, TOK_DEV, TOP)
    grad_all = grad_out.reshape(N_FSDP, TOK_DEV, model_width)

    def panel(total, inputs):
        hid, route_part, prob_part, grad_part = inputs
        row_of, valid, block_exp, row_tok, row_live, row_prob = route_layout(route_part, prob_part, expert_count, BLOCK, ROWS)
        safe_exp = jnp.maximum(block_exp, 0)
        prob_valid = prob_part * valid.astype(prob_part.dtype)
        routed = jnp.where(row_live[:, None] > 0, grad_part[row_tok], jnp.zeros((), grad_part.dtype))
        scaled = (row_prob[:, None] * routed.astype(jnp.float32)).astype(jnp.bfloat16)
        hid_blocks = hid.reshape(NBLK, BLOCK, unit_count)
        routed_blocks = routed.reshape(NBLK, BLOCK, model_width)

        def one_group(index):
            hid_group = lax.dynamic_slice_in_dim(hid_blocks, index * group, group, 2)
            weight_group = lax.dynamic_slice_in_dim(w_down, index * group, group, 2)
            chosen = jnp.take(weight_group, safe_exp, axis=1).astype(jnp.float32)
            out_rows = jnp.einsum('bri,dbi->brd', hid_group.astype(jnp.float32), chosen).reshape(ROWS, model_width)
            part = jnp.sum(prob_valid[:, :, None] * out_rows[row_of], axis=1).astype(jnp.bfloat16)
            back = jnp.einsum('brd,dbi->bri', routed_blocks.astype(jnp.float32), chosen).reshape(ROWS, group)
            return part, back

        parts, backs = lax.map(one_group, jnp.arange(N_EP, dtype=jnp.int32))
        combined = jnp.sum(parts.astype(jnp.float32), axis=0).astype(jnp.bfloat16)
        hidden_back = jnp.transpose(backs, (1, 0, 2)).reshape(ROWS, unit_count)
        grad_hid = (row_prob[:, None] * hidden_back).astype(jnp.bfloat16)
        row_dot = jnp.sum(hid.astype(jnp.float32) * hidden_back, axis=1)
        grad_prob = valid.astype(row_dot.dtype) * row_dot[row_of]
        row_exp = jnp.repeat(block_exp, BLOCK)
        member = (row_exp[:, None] == jnp.arange(expert_count, dtype=jnp.int32)[None, :]).astype(jnp.float32)
        masked = hid.astype(jnp.float32)[:, None, :] * member[:, :, None]
        term = jnp.einsum('rd,rei->dei', scaled.astype(jnp.float32), masked).astype(jnp.bfloat16)
        return total + term.astype(jnp.float32), (combined, grad_hid, grad_prob)

    start = jnp.zeros((model_width, expert_count, unit_count), jnp.float32)
    total, (combined, grad_hid, grad_prob) = lax.scan(panel, start, (hidden_all, route_all, prob_all, grad_all))
    output = combined.reshape(N_FSDP * TOK_DEV, model_width)
    grad_hidden = grad_hid.reshape(N_FSDP * ROWS, unit_count)
    grad_probs = grad_prob.reshape(N_FSDP * TOK_DEV, TOP)
    return output, grad_hidden, total.astype(jnp.bfloat16), grad_probs
```

```python
import jax
import jax.numpy as jnp
from jax import lax
from jax.sharding import PartitionSpec as P

F32 = jnp.float32
BF16 = jnp.bfloat16


def route_maps(route_ids, probs, experts):
    tokens = route_ids.shape[0]
    names = jnp.arange(experts, dtype=jnp.int32)
    hits = (route_ids[:, :, None] == names[None, None, :]).astype(F32)
    named = jnp.sum(hits, axis=1)
    place = jnp.arange(tokens, dtype=jnp.int32)
    earlier = (place[None, :] < place[:, None]).astype(F32)
    rank = jnp.sum(earlier[:, :, None] * named[None, :, :], axis=1).astype(jnp.int32)
    token_prob = jnp.sum(hits * probs[:, :, None], axis=1)
    owns = (rank.T[:, :, None] == place[None, None, :]) & (named.T[:, :, None] > 0)
    return hits, token_prob, owns.astype(BF16)


def local(hidden, w_down, route_ids, probs, grad_out):
    rows, units = hidden.shape
    experts = w_down.shape[1]
    tokens = route_ids.shape[0]
    hits, token_prob, owns = route_maps(route_ids, probs, experts)
    hid_tok = jnp.einsum(
        "etr,erf->tef", owns, hidden.reshape(experts, tokens, units), preferred_element_type=F32
    )
    scaled = (token_prob[:, :, None] * hid_tok).astype(BF16)
    hid_all = lax.all_gather(scaled, "fsdp", axis=0, tiled=True)
    grads = lax.all_gather(grad_out, "ep", axis=1, tiled=True)
    grads = lax.all_to_all(grads, "fsdp", split_axis=1, concat_axis=0, tiled=True)
    back_part = jnp.einsum("td,def->tef", grads, w_down, preferred_element_type=F32).astype(BF16)
    back = lax.psum_scatter(back_part, "fsdp", scatter_dimension=0, tiled=True)
    part = jnp.einsum("tef,def->td", hid_all, w_down, preferred_element_type=F32).astype(BF16)
    part = lax.all_to_all(part, "fsdp", split_axis=0, concat_axis=1, tiled=True)
    output = lax.psum_scatter(part, "ep", scatter_dimension=1, tiled=True)
    grad_weight = jnp.einsum("td,tef->def", grads, hid_all, preferred_element_type=F32).astype(BF16)
    back = back.astype(F32)
    grad_tok = (token_prob[:, :, None] * back).astype(BF16)
    grad_hidden = jnp.einsum("etr,tef->erf", owns, grad_tok, preferred_element_type=F32)
    grad_hidden = grad_hidden.astype(BF16).reshape(rows, units)
    dots = jnp.sum(hid_tok * back, axis=2)
    grad_probs = lax.psum(jnp.sum(hits * dots[:, None, :], axis=2), "ep")
    return (output, grad_hidden, grad_weight, grad_probs)


def solution(mesh):
    placed = (
        P("fsdp", "ep"),
        P("fsdp", None, "ep"),
        P("fsdp", None),
        P("fsdp", None),
        P("fsdp", "ep"),
    )
    return jax.shard_map(
        local,
        mesh=mesh,
        in_specs=placed,
        out_specs=(P("fsdp", "ep"), P("fsdp", "ep"), P("fsdp", None, "ep"), P("fsdp", None)),
        check_vma=False,
    )
```

```python
import functools

import jax
import jax.numpy as jnp
from jax import lax
from jax.experimental import pallas as pl
from jax.experimental.layout import Layout, with_layout_constraint
from jax.experimental.pallas import tpu as pltpu
from jax.sharding import PartitionSpec as P

F32 = jnp.float32
BF16 = jnp.bfloat16
MESH = pl.DeviceIdType.MESH
VMEM = pl.BlockSpec(memory_space=pltpu.VMEM)


def meet(n_fsdp, n_ep, p, z):
    barrier = pltpu.get_barrier_semaphore()
    for s in range(1, n_ep):
        pl.semaphore_signal(
            barrier, inc=1, device_id=(p, lax.rem(z + s, n_ep)), device_id_type=MESH
        )
    for s in range(1, n_fsdp):
        pl.semaphore_signal(
            barrier, inc=1, device_id=(lax.rem(p + s, n_fsdp), z), device_id_type=MESH
        )
    pl.semaphore_wait(barrier, n_ep - 1 + n_fsdp - 1)


def remote(src, dst, send, recv, to):
    return pltpu.make_async_remote_copy(
        src_ref=src, dst_ref=dst, send_sem=send, recv_sem=recv, device_id=to, device_id_type=MESH
    )


def spread_kernel(n_fsdp, n_ep, g_ref, out_ref, held, zsend, zrecv, psend, precv):
    ratio = g_ref.shape[0]
    p, z = lax.axis_index("fsdp"), lax.axis_index("ep")
    meet(n_fsdp, n_ep, p, z)
    along = []
    for s in range(1, n_ep):
        copy = remote(g_ref, held.at[z], zsend.at[s], zrecv.at[z], (p, lax.rem(z + s, n_ep)))
        copy.start()
        along.append(copy)
    for s in range(n_ep):
        q = lax.rem(z + n_ep - s, n_ep)
        if s:
            remote(g_ref, held.at[q], zsend.at[s], zrecv.at[q], (p, z)).wait_recv()
        for r in range(ratio):
            block = held.at[q, r] if s else g_ref.at[r]
            i = q * ratio + r

            @pl.when(i != p)
            def _():
                remote(block, out_ref.at[p], psend.at[s, r], precv.at[p], (i, z)).start()

            @pl.when(i == p)
            def _():
                out_ref[p] = block[...]

    for s in range(n_ep):
        q = lax.rem(z + n_ep - s, n_ep)
        for r in range(ratio):
            block = held.at[q, r] if s else g_ref.at[r]
            i = q * ratio + r

            @pl.when(i != p)
            def _():
                remote(block, out_ref.at[p], psend.at[s, r], precv.at[p], (i, z)).wait_send()

    for s in range(1, n_fsdp):
        f = lax.rem(p + s, n_fsdp)
        remote(g_ref.at[0], out_ref.at[f], psend.at[0, 0], precv.at[f], (f, z)).wait_recv()
    for copy in along:
        copy.wait_send()


def collect_kernel(n_fsdp, n_ep, part_ref, out_ref, held, sums, psend, precv, zsend, zrecv):
    ratio = out_ref.shape[0]
    p, z = lax.axis_index("fsdp"), lax.axis_index("ep")
    meet(n_fsdp, n_ep, p, z)
    held[p] = part_ref[p]
    across = []
    for s in range(1, n_fsdp):
        i = lax.rem(p + s, n_fsdp)
        copy = remote(part_ref.at[i], held.at[p], psend.at[s], precv.at[p], (i, z))
        copy.start()
        across.append(copy)
    along = []
    for s in range(1, n_ep + 1):
        q = lax.rem(z + s, n_ep)
        for r in range(ratio):
            f = q * ratio + r

            @pl.when(f != p)
            def _():
                remote(part_ref.at[0], held.at[f], psend.at[0], precv.at[f], (p, z)).wait_recv()

        if s < n_ep:
            copy = remote(
                held.at[pl.ds(q * ratio, ratio)], sums.at[z], zsend.at[s], zrecv.at[z], (p, q)
            )
            copy.start()
            along.append(copy)
    total = held[pl.ds(z * ratio, ratio)].astype(F32)
    for s in range(1, n_ep):
        q = lax.rem(z + s, n_ep)
        remote(
            held.at[pl.ds(q * ratio, ratio)], sums.at[q], zsend.at[s], zrecv.at[q], (p, q)
        ).wait_recv()
        total = total + sums[q].astype(F32)
    out_ref[...] = total.astype(BF16)
    for copy in across + along:
        copy.wait_send()


def add_kernel(n_ep, x_ref, out_ref, held, send, recv):
    p, z = lax.axis_index("fsdp"), lax.axis_index("ep")
    meet(1, n_ep, p, z)
    copies = []
    for s in range(1, n_ep):
        copy = remote(x_ref, held.at[z], send.at[s], recv.at[z], (p, lax.rem(z + s, n_ep)))
        copy.start()
        copies.append(copy)
    total = x_ref[...]
    for s in range(1, n_ep):
        q = lax.rem(z + s, n_ep)
        remote(x_ref, held.at[q], send.at[s], recv.at[q], (p, q)).wait_recv()
        total = total + held[q]
    out_ref[...] = total
    for copy in copies:
        copy.wait_send()


def talk(body, key, x, shape, scratch, flops=0):
    return pl.pallas_call(
        body,
        out_shape=jax.ShapeDtypeStruct(shape, x.dtype),
        in_specs=[VMEM],
        out_specs=VMEM,
        scratch_shapes=scratch,
        cost_estimate=pl.CostEstimate(flops=flops, bytes_accessed=100_000_000, transcendentals=0),
        compiler_params=pltpu.CompilerParams(collective_id=key, has_side_effects=True),
    )(x)


def spread(grad_out, n_fsdp, n_ep):
    tokens, width = grad_out.shape
    ratio = n_fsdp // n_ep
    cut = width // ratio
    blocks = jnp.stack([grad_out[:, r * cut : (r + 1) * cut] for r in range(ratio)])
    dma = pltpu.SemaphoreType.DMA
    out = talk(
        functools.partial(spread_kernel, n_fsdp, n_ep),
        0,
        blocks,
        (n_fsdp, tokens, cut),
        [
            pltpu.VMEM((n_ep, ratio, tokens, cut), BF16),
            dma((n_ep,)),
            dma((n_ep,)),
            dma((n_ep, ratio)),
            dma((n_fsdp,)),
        ],
    )
    return out.reshape(n_fsdp * tokens, cut)


def collect(part, n_fsdp, n_ep):
    cut = part.shape[1]
    tokens = part.shape[0] // n_fsdp
    ratio = n_fsdp // n_ep
    dma = pltpu.SemaphoreType.DMA
    out = talk(
        functools.partial(collect_kernel, n_fsdp, n_ep),
        1,
        part.reshape(n_fsdp, tokens, cut),
        (ratio, tokens, cut),
        [
            pltpu.VMEM((n_fsdp, tokens, cut), BF16),
            pltpu.VMEM((n_ep, ratio, tokens, cut), BF16),
            dma((n_fsdp,)),
            dma((n_fsdp,)),
            dma((n_ep,)),
            dma((n_ep,)),
        ],
    )
    return jnp.concatenate([out[r] for r in range(ratio)], axis=1)


def add_up(x, n_ep):
    dma = pltpu.SemaphoreType.DMA
    return talk(
        functools.partial(add_kernel, n_ep),
        2,
        x,
        x.shape,
        [pltpu.VMEM((n_ep,) + x.shape, F32), dma((n_ep,)), dma((n_ep,))],
    )


def route_maps(route_ids, probs, experts):
    tokens = route_ids.shape[0]
    names = jnp.arange(experts, dtype=jnp.int32)
    hits = (route_ids[:, :, None] == names[None, None, :]).astype(F32)
    named = jnp.sum(hits, axis=1)
    place = jnp.arange(tokens, dtype=jnp.int32)
    earlier = (place[None, :] < place[:, None]).astype(F32)
    rank = jnp.sum(earlier[:, :, None] * named[None, :, :], axis=1).astype(jnp.int32)
    token_prob = jnp.sum(hits * probs[:, :, None], axis=1)
    owns = (rank.T[:, :, None] == place[None, None, :]) & (named.T[:, :, None] > 0)
    return hits, token_prob, owns.astype(BF16)


def local(n_fsdp, n_ep, hidden, w_down, route_ids, probs, grad_out):
    rows, units = hidden.shape
    experts = w_down.shape[1]
    tokens = route_ids.shape[0]
    hits, token_prob, owns = route_maps(route_ids, probs, experts)
    hid_tok = jnp.einsum(
        "etr,erf->tef", owns, hidden.reshape(experts, tokens, units), preferred_element_type=F32
    )
    scaled = (token_prob[:, :, None] * hid_tok).astype(BF16)
    hid_tok = hid_tok.astype(BF16)
    hid_all = lax.all_gather(scaled, "fsdp", axis=0, tiled=True)
    grads = spread(grad_out, n_fsdp, n_ep)
    back_part = jnp.einsum("td,def->tef", grads, w_down, preferred_element_type=F32).astype(BF16)
    hid_all, back_part = lax.optimization_barrier((hid_all, back_part))
    back = lax.psum_scatter(back_part, "fsdp", scatter_dimension=0, tiled=True)
    part = jnp.einsum("tef,def->td", hid_all, w_down, preferred_element_type=F32).astype(BF16)
    output = collect(part, n_fsdp, n_ep)
    grad_weight = jnp.stack(
        [
            jnp.einsum("td,tf->df", grads, hid_all[:, e], preferred_element_type=F32).astype(BF16)
            for e in range(experts)
        ],
        axis=1,
    )
    grad_weight = with_layout_constraint(grad_weight, Layout(major_to_minor=(0, 1, 2)))
    back, output, grad_weight = lax.optimization_barrier((back, output, grad_weight))
    back = back.astype(F32)
    dots = jnp.sum(hid_tok.astype(F32) * back, axis=2)
    dots = add_up(dots.T, n_ep).T
    grad_tok = (token_prob[:, :, None] * back).astype(BF16)
    grad_hidden = jnp.einsum("etr,tef->erf", owns, grad_tok, preferred_element_type=F32)
    grad_hidden = grad_hidden.astype(BF16).reshape(rows, units)
    grad_probs = jnp.sum(hits * dots[:, None, :], axis=2)
    return (output, grad_hidden, grad_weight, grad_probs)


def solution(mesh):
    placed = (
        P("fsdp", "ep"),
        P("fsdp", None, "ep"),
        P("fsdp", None),
        P("fsdp", None),
        P("fsdp", "ep"),
    )
    return jax.shard_map(
        functools.partial(local, mesh.shape["fsdp"], mesh.shape["ep"]),
        mesh=mesh,
        in_specs=placed,
        out_specs=(P("fsdp", "ep"), P("fsdp", "ep"), P("fsdp", None, "ep"), P("fsdp", None)),
        check_vma=False,
    )
```

```python
import functools

import jax
import jax.numpy as jnp
from jax import lax
from jax.experimental import pallas as pl
from jax.experimental.layout import Layout, with_layout_constraint
from jax.experimental.pallas import tpu as pltpu
from jax.sharding import PartitionSpec as P

F32 = jnp.float32
BF16 = jnp.bfloat16
MESH = pl.DeviceIdType.MESH
VMEM = pl.BlockSpec(memory_space=pltpu.VMEM)


def meet(n_fsdp, n_ep, p, z):
    barrier = pltpu.get_barrier_semaphore()
    for s in range(1, n_ep):
        pl.semaphore_signal(
            barrier, inc=1, device_id=(p, lax.rem(z + s, n_ep)), device_id_type=MESH
        )
    for s in range(1, n_fsdp):
        pl.semaphore_signal(
            barrier, inc=1, device_id=(lax.rem(p + s, n_fsdp), z), device_id_type=MESH
        )
    pl.semaphore_wait(barrier, n_ep - 1 + n_fsdp - 1)


def remote(src, dst, send, recv, to):
    return pltpu.make_async_remote_copy(
        src_ref=src, dst_ref=dst, send_sem=send, recv_sem=recv, device_id=to, device_id_type=MESH
    )


def spread_kernel(
    n_fsdp, n_ep, g_ref, h_ref, out_ref, hall_ref, held, zsend, zrecv, psend, precv, hsend, fsend, hrecv, own
):
    ratio = g_ref.shape[0]
    n_chip = n_fsdp // 2
    p, z = lax.axis_index("fsdp"), lax.axis_index("ep")
    chip, core = lax.div(p, 2), lax.rem(p, 2)
    mate = chip * 2 + 1 - core
    meet(n_fsdp, n_ep, p, z)
    sends = []
    for s in range(1, n_ep):
        copy = remote(g_ref, held.at[z], zsend.at[s], zrecv.at[z], (p, lax.rem(z + s, n_ep)))
        copy.start()
        sends.append(copy)
    keep = pltpu.make_async_copy(h_ref, hall_ref.at[:, p], own)
    keep.start()

    def pieces(s, act):
        q = lax.rem(z + n_ep - s, n_ep)
        for r in range(ratio):
            block = held.at[q, r] if s else g_ref.at[r]
            i = q * ratio + r

            @pl.when(i != p)
            def _():
                act(remote(block, out_ref.at[p], psend.at[s, r], precv.at[p], (i, z)))

            if act is begin:

                @pl.when(i == p)
                def _():
                    out_ref[p] = block[...]

    def begin(copy):
        copy.start()

    def end(copy):
        copy.wait_send()

    pieces(0, begin)
    for s in range(1, n_chip):
        to = lax.rem(chip + s, n_chip) * 2 + core
        copy = remote(h_ref, hall_ref.at[:, p], hsend.at[s], hrecv.at[p], (to, z))
        copy.start()
        sends.append(copy)
    copy = remote(h_ref, hall_ref.at[:, p], hsend.at[0], hrecv.at[p], (mate, z))
    copy.start()
    sends.append(copy)
    for s in range(1, max(n_ep, n_chip)):
        if s < n_ep:
            q = lax.rem(z + n_ep - s, n_ep)
            remote(g_ref, held.at[q], zsend.at[s], zrecv.at[q], (p, z)).wait_recv()
            pieces(s, begin)
        if s < n_chip:
            f = lax.rem(chip + n_chip - s, n_chip) * 2 + core
            copy = remote(hall_ref.at[:, f], hall_ref.at[:, f], fsend.at[s], hrecv.at[f], (mate, z))
            copy.wait_recv()
            copy.start()
            sends.append(copy)
    for s in range(n_chip):
        f = lax.rem(chip + s, n_chip) * 2 + 1 - core
        remote(h_ref, hall_ref.at[:, f], hsend.at[0], hrecv.at[f], (mate, z)).wait_recv()
    for s in range(1, n_fsdp):
        f = lax.rem(p + s, n_fsdp)
        remote(g_ref.at[0], out_ref.at[f], psend.at[0, 0], precv.at[f], (f, z)).wait_recv()
    for s in range(n_ep):
        pieces(s, end)
    for copy in sends:
        copy.wait_send()
    keep.wait()


def collect_kernel(n_fsdp, n_ep, part_ref, out_ref, held, sums, psend, precv, zsend, zrecv):
    ratio = out_ref.shape[0]
    p, z = lax.axis_index("fsdp"), lax.axis_index("ep")
    meet(n_fsdp, n_ep, p, z)
    held[p] = part_ref[p]
    across = []
    for s in range(1, n_fsdp):
        i = lax.rem(p + s, n_fsdp)
        copy = remote(part_ref.at[i], held.at[p], psend.at[s], precv.at[p], (i, z))
        copy.start()
        across.append(copy)
    along = []
    for s in range(1, n_ep + 1):
        q = lax.rem(z + s, n_ep)
        for r in range(ratio):
            f = q * ratio + r

            @pl.when(f != p)
            def _():
                remote(part_ref.at[0], held.at[f], psend.at[0], precv.at[f], (p, z)).wait_recv()

        if s < n_ep:
            copy = remote(
                held.at[pl.ds(q * ratio, ratio)], sums.at[z], zsend.at[s], zrecv.at[z], (p, q)
            )
            copy.start()
            along.append(copy)
    total = held[pl.ds(z * ratio, ratio)].astype(F32)
    for s in range(1, n_ep):
        q = lax.rem(z + s, n_ep)
        remote(
            held.at[pl.ds(q * ratio, ratio)], sums.at[q], zsend.at[s], zrecv.at[q], (p, q)
        ).wait_recv()
        total = total + sums[q].astype(F32)
    out_ref[...] = total.astype(BF16)
    for copy in across + along:
        copy.wait_send()


def add_kernel(n_ep, x_ref, out_ref, held, send, recv):
    p, z = lax.axis_index("fsdp"), lax.axis_index("ep")
    meet(1, n_ep, p, z)
    copies = []
    for s in range(1, n_ep):
        copy = remote(x_ref, held.at[z], send.at[s], recv.at[z], (p, lax.rem(z + s, n_ep)))
        copy.start()
        copies.append(copy)
    total = x_ref[...]
    for s in range(1, n_ep):
        q = lax.rem(z + s, n_ep)
        remote(x_ref, held.at[q], send.at[s], recv.at[q], (p, q)).wait_recv()
        total = total + held[q]
    out_ref[...] = total
    for copy in copies:
        copy.wait_send()


def talk(body, key, x, shape, scratch, flops=0):
    return pl.pallas_call(
        body,
        out_shape=jax.ShapeDtypeStruct(shape, x.dtype),
        in_specs=[VMEM],
        out_specs=VMEM,
        scratch_shapes=scratch,
        cost_estimate=pl.CostEstimate(flops=flops, bytes_accessed=100_000_000, transcendentals=0),
        compiler_params=pltpu.CompilerParams(collective_id=key, has_side_effects=True),
    )(x)


def spread(grad_out, scaled, n_fsdp, n_ep):
    tokens, width = grad_out.shape
    experts, _, units = scaled.shape
    ratio = n_fsdp // n_ep
    cut = width // ratio
    blocks = jnp.stack([grad_out[:, r * cut : (r + 1) * cut] for r in range(ratio)])
    dma = pltpu.SemaphoreType.DMA
    anywhere = pl.BlockSpec(memory_space=pl.ANY)
    out, hid_all = pl.pallas_call(
        functools.partial(spread_kernel, n_fsdp, n_ep),
        out_shape=(
            jax.ShapeDtypeStruct((n_fsdp, tokens, cut), BF16),
            jax.ShapeDtypeStruct((experts, n_fsdp, tokens, units), BF16),
        ),
        in_specs=[VMEM, anywhere],
        out_specs=(VMEM, anywhere),
        scratch_shapes=[
            pltpu.VMEM((n_ep, ratio, tokens, cut), BF16),
            dma((n_ep,)),
            dma((n_ep,)),
            dma((n_ep, ratio)),
            dma((n_fsdp,)),
            dma((n_fsdp // 2,)),
            dma((n_fsdp // 2,)),
            dma((n_fsdp,)),
            dma,
        ],
        compiler_params=pltpu.CompilerParams(collective_id=0, has_side_effects=True),
    )(blocks, scaled)
    return out.reshape(n_fsdp * tokens, cut), hid_all.reshape(experts, n_fsdp * tokens, units)


def collect(part, n_fsdp, n_ep):
    cut = part.shape[1]
    tokens = part.shape[0] // n_fsdp
    ratio = n_fsdp // n_ep
    dma = pltpu.SemaphoreType.DMA
    out = talk(
        functools.partial(collect_kernel, n_fsdp, n_ep),
        1,
        part.reshape(n_fsdp, tokens, cut),
        (ratio, tokens, cut),
        [
            pltpu.VMEM((n_fsdp, tokens, cut), BF16),
            pltpu.VMEM((n_ep, ratio, tokens, cut), BF16),
            dma((n_fsdp,)),
            dma((n_fsdp,)),
            dma((n_ep,)),
            dma((n_ep,)),
        ],
    )
    return jnp.concatenate([out[r] for r in range(ratio)], axis=1)


def add_up(x, n_ep):
    dma = pltpu.SemaphoreType.DMA
    return talk(
        functools.partial(add_kernel, n_ep),
        2,
        x,
        x.shape,
        [pltpu.VMEM((n_ep,) + x.shape, F32), dma((n_ep,)), dma((n_ep,))],
    )


def route_maps(route_ids, probs, experts):
    tokens = route_ids.shape[0]
    names = jnp.arange(experts, dtype=jnp.int32)
    hits = (route_ids[:, :, None] == names[None, None, :]).astype(F32)
    named = jnp.sum(hits, axis=1)
    place = jnp.arange(tokens, dtype=jnp.int32)
    earlier = (place[None, :] < place[:, None]).astype(F32)
    rank = jnp.sum(earlier[:, :, None] * named[None, :, :], axis=1).astype(jnp.int32)
    token_prob = jnp.sum(hits * probs[:, :, None], axis=1)
    owns = (rank.T[:, :, None] == place[None, None, :]) & (named.T[:, :, None] > 0)
    return hits, token_prob, owns.astype(BF16)


def local(n_fsdp, n_ep, hidden, w_down, route_ids, probs, grad_out):
    rows, units = hidden.shape
    experts = w_down.shape[1]
    tokens = route_ids.shape[0]
    hits, token_prob, owns = route_maps(route_ids, probs, experts)
    hid_tok = jnp.einsum(
        "etr,erf->etf", owns, hidden.reshape(experts, tokens, units), preferred_element_type=F32
    )
    scaled = (token_prob.T[:, :, None] * hid_tok).astype(BF16)
    hid_tok = hid_tok.astype(BF16)
    grads, hid_all = spread(grad_out, scaled, n_fsdp, n_ep)
    back_part = jnp.einsum("td,def->tef", grads, w_down, preferred_element_type=F32).astype(BF16)
    hid_all, back_part = lax.optimization_barrier((hid_all, back_part))
    back = lax.psum_scatter(back_part, "fsdp", scatter_dimension=0, tiled=True)
    part = jnp.einsum("etf,def->td", hid_all, w_down, preferred_element_type=F32).astype(BF16)
    output = collect(part, n_fsdp, n_ep)
    grad_weight = jnp.einsum("td,etf->def", grads, hid_all, preferred_element_type=F32).astype(BF16)
    grad_weight = with_layout_constraint(grad_weight, Layout(major_to_minor=(0, 1, 2)))
    back, output, grad_weight = lax.optimization_barrier((back, output, grad_weight))
    back = back.astype(F32)
    dots = jnp.sum(hid_tok.transpose(1, 0, 2).astype(F32) * back, axis=2)
    dots = add_up(dots.T, n_ep).T
    grad_tok = (token_prob[:, :, None] * back).astype(BF16)
    grad_hidden = jnp.einsum("etr,tef->erf", owns, grad_tok, preferred_element_type=F32)
    grad_hidden = grad_hidden.astype(BF16).reshape(rows, units)
    grad_probs = jnp.sum(hits * dots[:, None, :], axis=2)
    return (output, grad_hidden, grad_weight, grad_probs)


def solution(mesh):
    placed = (
        P("fsdp", "ep"),
        P("fsdp", None, "ep"),
        P("fsdp", None),
        P("fsdp", None),
        P("fsdp", "ep"),
    )
    return jax.shard_map(
        functools.partial(local, mesh.shape["fsdp"], mesh.shape["ep"]),
        mesh=mesh,
        in_specs=placed,
        out_specs=(P("fsdp", "ep"), P("fsdp", "ep"), P("fsdp", None, "ep"), P("fsdp", None)),
        check_vma=False,
    )
```

```python
import functools

import jax
import jax.numpy as jnp
from jax import lax
from jax.experimental import pallas as pl
from jax.experimental.layout import Layout, with_layout_constraint
from jax.experimental.pallas import tpu as pltpu
from jax.sharding import PartitionSpec as P

F32 = jnp.float32
BF16 = jnp.bfloat16
MESH = pl.DeviceIdType.MESH
VMEM = pl.BlockSpec(memory_space=pltpu.VMEM)


def meet(n_fsdp, n_ep, p, z):
    barrier = pltpu.get_barrier_semaphore()
    for s in range(1, n_ep):
        pl.semaphore_signal(
            barrier, inc=1, device_id=(p, lax.rem(z + s, n_ep)), device_id_type=MESH
        )
    for s in range(1, n_fsdp):
        pl.semaphore_signal(
            barrier, inc=1, device_id=(lax.rem(p + s, n_fsdp), z), device_id_type=MESH
        )
    pl.semaphore_wait(barrier, n_ep - 1 + n_fsdp - 1)


def remote(src, dst, send, recv, to):
    return pltpu.make_async_remote_copy(
        src_ref=src, dst_ref=dst, send_sem=send, recv_sem=recv, device_id=to, device_id_type=MESH
    )


def spread_kernel(
    n_fsdp, n_ep, g_ref, h_ref, out_ref, hall_ref, held, zsend, zrecv, psend, precv, hsend, fsend, hrecv, own
):
    ratio = g_ref.shape[0]
    n_chip = n_fsdp // 2
    p, z = lax.axis_index("fsdp"), lax.axis_index("ep")
    chip, core = lax.div(p, 2), lax.rem(p, 2)
    mate = chip * 2 + 1 - core
    rows_half = h_ref.shape[1] // 2

    def around(c):
        wide = n_chip // 2
        return c + lax.div(c, wide) * (3 * wide - 1 - 2 * c)

    meet(n_fsdp, n_ep, p, z)
    sends = []
    for s in range(1, n_ep):
        copy = remote(g_ref, held.at[z], zsend.at[s], zrecv.at[z], (p, lax.rem(z + s, n_ep)))
        copy.start()
        sends.append(copy)
    keep = pltpu.make_async_copy(h_ref, hall_ref.at[:, p], own)
    keep.start()

    def pieces(s, act):
        q = lax.rem(z + n_ep - s, n_ep)
        for r in range(ratio):
            block = held.at[q, r] if s else g_ref.at[r]
            i = q * ratio + r

            @pl.when(i != p)
            def _():
                act(remote(block, out_ref.at[p], psend.at[s, r], precv.at[p], (i, z)))

            if act is begin:

                @pl.when(i == p)
                def _():
                    out_ref[p] = block[...]

    def begin(copy):
        copy.start()

    def end(copy):
        copy.wait_send()

    pieces(0, begin)
    place = around(chip)
    after = around(lax.rem(place + 1, n_chip)) * 2 + core
    before = around(lax.rem(place + n_chip - 1, n_chip)) * 2 + core

    def relay(s):
        for half, to in ((0, after), (1, before)):
            step = n_chip - s if half == 0 else s
            f = around(lax.rem(place + step, n_chip)) * 2 + core
            rows = pl.ds(half * rows_half, rows_half)
            there = hall_ref.at[:, f, rows]
            src = there if s else h_ref.at[:, rows]
            if s:
                remote(src, there, hsend.at[half, s], hrecv.at[half, f], (to, z)).wait_recv()
            if s < n_chip - 1:
                copy = remote(src, there, hsend.at[half, s], hrecv.at[half, f], (to, z))
                copy.start()
                sends.append(copy)
            copy = remote(src, there, fsend.at[half, s], hrecv.at[half, f], (mate, z))
            copy.start()
            sends.append(copy)

    relay(0)
    for s in range(1, max(n_ep, n_chip)):
        if s < n_chip:
            relay(s)
        if s < n_ep:
            q = lax.rem(z + n_ep - s, n_ep)
            remote(g_ref, held.at[q], zsend.at[s], zrecv.at[q], (p, z)).wait_recv()
            pieces(s, begin)
    for s in range(n_chip):
        f = lax.rem(chip + s, n_chip) * 2 + 1 - core
        for half in range(2):
            rows = pl.ds(half * rows_half, rows_half)
            there = hall_ref.at[:, f, rows]
            remote(there, there, fsend.at[half, 0], hrecv.at[half, f], (mate, z)).wait_recv()
    for s in range(1, n_fsdp):
        f = lax.rem(p + s, n_fsdp)
        remote(g_ref.at[0], out_ref.at[f], psend.at[0, 0], precv.at[f], (f, z)).wait_recv()
    for s in range(n_ep):
        pieces(s, end)
    for copy in sends:
        copy.wait_send()
    keep.wait()


def collect_kernel(n_fsdp, n_ep, part_ref, out_ref, held, sums, psend, precv, zsend, zrecv):
    ratio = out_ref.shape[0]
    p, z = lax.axis_index("fsdp"), lax.axis_index("ep")
    meet(n_fsdp, n_ep, p, z)
    held[p] = part_ref[p]
    across = []
    for s in range(1, n_fsdp):
        i = lax.rem(p + s, n_fsdp)
        copy = remote(part_ref.at[i], held.at[p], psend.at[s], precv.at[p], (i, z))
        copy.start()
        across.append(copy)
    along = []
    for s in range(1, n_ep + 1):
        q = lax.rem(z + s, n_ep)
        for r in range(ratio):
            f = q * ratio + r

            @pl.when(f != p)
            def _():
                remote(part_ref.at[0], held.at[f], psend.at[0], precv.at[f], (p, z)).wait_recv()

        if s < n_ep:
            copy = remote(
                held.at[pl.ds(q * ratio, ratio)], sums.at[z], zsend.at[s], zrecv.at[z], (p, q)
            )
            copy.start()
            along.append(copy)
    total = held[pl.ds(z * ratio, ratio)].astype(F32)
    for s in range(1, n_ep):
        q = lax.rem(z + s, n_ep)
        remote(
            held.at[pl.ds(q * ratio, ratio)], sums.at[q], zsend.at[s], zrecv.at[q], (p, q)
        ).wait_recv()
        total = total + sums[q].astype(F32)
    out_ref[...] = total.astype(BF16)
    for copy in across + along:
        copy.wait_send()


def add_kernel(n_ep, x_ref, out_ref, held, send, recv):
    p, z = lax.axis_index("fsdp"), lax.axis_index("ep")
    meet(1, n_ep, p, z)
    copies = []
    for s in range(1, n_ep):
        copy = remote(x_ref, held.at[z], send.at[s], recv.at[z], (p, lax.rem(z + s, n_ep)))
        copy.start()
        copies.append(copy)
    total = x_ref[...]
    for s in range(1, n_ep):
        q = lax.rem(z + s, n_ep)
        remote(x_ref, held.at[q], send.at[s], recv.at[q], (p, q)).wait_recv()
        total = total + held[q]
    out_ref[...] = total
    for copy in copies:
        copy.wait_send()


def talk(body, key, x, shape, scratch, flops=0):
    return pl.pallas_call(
        body,
        out_shape=jax.ShapeDtypeStruct(shape, x.dtype),
        in_specs=[VMEM],
        out_specs=VMEM,
        scratch_shapes=scratch,
        cost_estimate=pl.CostEstimate(flops=flops, bytes_accessed=100_000_000, transcendentals=0),
        compiler_params=pltpu.CompilerParams(collective_id=key, has_side_effects=True),
    )(x)


def spread(grad_out, scaled, n_fsdp, n_ep):
    tokens, width = grad_out.shape
    experts, _, units = scaled.shape
    ratio = n_fsdp // n_ep
    cut = width // ratio
    blocks = jnp.stack([grad_out[:, r * cut : (r + 1) * cut] for r in range(ratio)])
    dma = pltpu.SemaphoreType.DMA
    anywhere = pl.BlockSpec(memory_space=pl.ANY)
    out, hid_all = pl.pallas_call(
        functools.partial(spread_kernel, n_fsdp, n_ep),
        out_shape=(
            jax.ShapeDtypeStruct((n_fsdp, tokens, cut), BF16),
            jax.ShapeDtypeStruct((experts, n_fsdp, tokens, units), BF16),
        ),
        in_specs=[VMEM, anywhere],
        out_specs=(VMEM, anywhere),
        scratch_shapes=[
            pltpu.VMEM((n_ep, ratio, tokens, cut), BF16),
            dma((n_ep,)),
            dma((n_ep,)),
            dma((n_ep, ratio)),
            dma((n_fsdp,)),
            dma((2, n_fsdp // 2)),
            dma((2, n_fsdp // 2)),
            dma((2, n_fsdp)),
            dma,
        ],
        compiler_params=pltpu.CompilerParams(collective_id=0, has_side_effects=True),
    )(blocks, scaled)
    return out.reshape(n_fsdp * tokens, cut), hid_all.reshape(experts, n_fsdp * tokens, units)


def collect(part, n_fsdp, n_ep):
    cut = part.shape[1]
    tokens = part.shape[0] // n_fsdp
    ratio = n_fsdp // n_ep
    dma = pltpu.SemaphoreType.DMA
    out = talk(
        functools.partial(collect_kernel, n_fsdp, n_ep),
        1,
        part.reshape(n_fsdp, tokens, cut),
        (ratio, tokens, cut),
        [
            pltpu.VMEM((n_fsdp, tokens, cut), BF16),
            pltpu.VMEM((n_ep, ratio, tokens, cut), BF16),
            dma((n_fsdp,)),
            dma((n_fsdp,)),
            dma((n_ep,)),
            dma((n_ep,)),
        ],
    )
    return jnp.concatenate([out[r] for r in range(ratio)], axis=1)


def add_up(x, n_ep):
    dma = pltpu.SemaphoreType.DMA
    return talk(
        functools.partial(add_kernel, n_ep),
        2,
        x,
        x.shape,
        [pltpu.VMEM((n_ep,) + x.shape, F32), dma((n_ep,)), dma((n_ep,))],
    )


def route_maps(route_ids, probs, experts):
    tokens = route_ids.shape[0]
    names = jnp.arange(experts, dtype=jnp.int32)
    hits = (route_ids[:, :, None] == names[None, None, :]).astype(F32)
    named = jnp.sum(hits, axis=1)
    place = jnp.arange(tokens, dtype=jnp.int32)
    earlier = (place[None, :] < place[:, None]).astype(F32)
    rank = jnp.sum(earlier[:, :, None] * named[None, :, :], axis=1).astype(jnp.int32)
    token_prob = jnp.sum(hits * probs[:, :, None], axis=1)
    owns = (rank.T[:, :, None] == place[None, None, :]) & (named.T[:, :, None] > 0)
    return hits, token_prob, owns.astype(BF16)


def local(n_fsdp, n_ep, hidden, w_down, route_ids, probs, grad_out):
    rows, units = hidden.shape
    experts = w_down.shape[1]
    tokens = route_ids.shape[0]
    hits, token_prob, owns = route_maps(route_ids, probs, experts)
    hid_tok = jnp.einsum(
        "etr,erf->etf", owns, hidden.reshape(experts, tokens, units), preferred_element_type=F32
    )
    scaled = (token_prob.T[:, :, None] * hid_tok).astype(BF16)
    hid_tok = hid_tok.astype(BF16)
    grads, hid_all = spread(grad_out, scaled, n_fsdp, n_ep)
    back_part = jnp.einsum("td,def->tef", grads, w_down, preferred_element_type=F32).astype(BF16)
    hid_all, back_part = lax.optimization_barrier((hid_all, back_part))
    back = lax.psum_scatter(back_part, "fsdp", scatter_dimension=0, tiled=True)
    part = jnp.einsum("etf,def->td", hid_all, w_down, preferred_element_type=F32).astype(BF16)
    output = collect(part, n_fsdp, n_ep)
    grad_weight = jnp.einsum("td,etf->def", grads, hid_all, preferred_element_type=F32).astype(BF16)
    grad_weight = with_layout_constraint(grad_weight, Layout(major_to_minor=(0, 1, 2)))
    back, output, grad_weight = lax.optimization_barrier((back, output, grad_weight))
    back = back.astype(F32)
    dots = jnp.sum(hid_tok.transpose(1, 0, 2).astype(F32) * back, axis=2)
    dots = add_up(dots.T, n_ep).T
    grad_tok = (token_prob[:, :, None] * back).astype(BF16)
    grad_hidden = jnp.einsum("etr,tef->erf", owns, grad_tok, preferred_element_type=F32)
    grad_hidden = grad_hidden.astype(BF16).reshape(rows, units)
    grad_probs = jnp.sum(hits * dots[:, None, :], axis=2)
    return (output, grad_hidden, grad_weight, grad_probs)


def solution(mesh):
    placed = (
        P("fsdp", "ep"),
        P("fsdp", None, "ep"),
        P("fsdp", None),
        P("fsdp", None),
        P("fsdp", "ep"),
    )
    return jax.shard_map(
        functools.partial(local, mesh.shape["fsdp"], mesh.shape["ep"]),
        mesh=mesh,
        in_specs=placed,
        out_specs=(P("fsdp", "ep"), P("fsdp", "ep"), P("fsdp", None, "ep"), P("fsdp", None)),
        check_vma=False,
    )
```
